256 devices in a mesh: row: 32 (over z, x_lo, core), col: 8 (over y, x_hi).
Axes of the slice: x: 4 (x_hi: 2, x_lo: 2; x = x_hi * 2 + x_lo), y: 4, z: 8, core: 2. Of those that a mesh axis runs over, the one named last changes fastest.
Arguments:
- matrix: float32 [8192, 4096], P('row', 'col'), may hold values from -12 to 12
Outputs:
- rotated: float32 [8192, 4096], P('row', 'col')
- coupling: float32 [2], replicated
The draws below stay inside these ranges and needn't reach their ends.
All inputs are finite; a program needn't handle non-finite values.
Results may differ from the reference program's by a relative error of at most 0.00027.
Values sent between devices are 32-bit elements; how exact they have to be, the bound alone decides.
No kernel may reach another device: no remote copies, remote signals or barrier semaphores. Data moves between devices by JAX's collectives and lax.ppermute only.
A program may use at most 64 MiB of HBM per device.

```python
import math
import jax
import jax.numpy as jnp
from jax import lax

BW = 256
STEPS = 2
NB = 16
ROWS = 8192


def draw_matrix(key, part):
    subkeys = jax.random.split(key, 4)
    column_index = jnp.arange(NB * BW, dtype=jnp.float32)[None, :] / (NB * BW)
    rising = jnp.exp(math.log(1.6) * column_index)
    spread = jnp.exp(jax.random.uniform(subkeys[0], (1, NB * BW), jnp.float32, 0.0, math.log(2.5)))
    loading = jax.random.uniform(subkeys[1], (1, NB * BW), jnp.float32, -1.0, 1.0) * (0.5 + column_index)
    common = jnp.clip(jax.random.normal(subkeys[2], (ROWS, 1), jnp.float32), -4.0, 4.0)
    noise_part = jax.random.normal(subkeys[3], (ROWS, NB * BW), jnp.float32)
    strength = 0.3
    combined = noise_part + 0.4 * jnp.roll(noise_part, 1, axis=1) + strength * common * loading
    return jnp.clip(combined * spread * rising, -12.0, 12.0)


def setup_inputs(seed: int = 0) -> dict:
    keys = jax.random.split(jax.random.key(seed), 2)
    matrix = draw_matrix(jax.random.fold_in(keys[1], 71), 0)
    return {"matrix": matrix}


def pair_rotation(pair_gram):
    lower_factor = jnp.linalg.cholesky(pair_gram)
    inner_gram = jnp.dot(lower_factor.T, lower_factor, precision=lax.Precision.HIGHEST)
    second = jnp.linalg.cholesky(inner_gram)
    return jax.scipy.linalg.solve_triangular(second, lower_factor.T, lower=True).T

def one_pair(blocks_pair):
    top_block, bottom_block = blocks_pair
    joined = jnp.concatenate([top_block, bottom_block], axis=1)
    pair_gram = jnp.dot(joined.T, joined, precision=lax.Precision.HIGHEST)
    diagonal = jnp.diagonal(pair_gram)
    cross = pair_gram[:BW, BW:]
    term = jnp.sum(cross * cross / (diagonal[:BW, None] * diagonal[None, BW:]))
    turned = jnp.dot(joined, pair_rotation(pair_gram), precision=lax.Precision.HIGHEST)
    return (turned[:, :BW], turned[:, BW:], term)

def reference(matrix):
    slots = NB // 2
    blocks = matrix.reshape(ROWS, slots, 2, BW)
    top_blocks = jnp.transpose(blocks[:, :, 0], (1, 0, 2))
    bottom_blocks = jnp.transpose(blocks[:, :, 1], (1, 0, 2))
    totals = []
    for step_index in range(STEPS):
        top_new, bottom_new, terms = lax.map(one_pair, (top_blocks, bottom_blocks))
        totals.append(jnp.sum(terms))
        top_blocks = jnp.concatenate([top_new[0:1], bottom_new[0:1], top_new[1:slots - 1]], axis=0)
        bottom_blocks = jnp.concatenate([bottom_new[1:], top_new[slots - 1:]], axis=0)
    coupling = jnp.sqrt(jnp.stack(totals) / (NB * BW // 2))
    stacked = jnp.stack([top_blocks, bottom_blocks], axis=1)
    rotated = jnp.transpose(stacked, (2, 0, 1, 3)).reshape(ROWS, NB * BW)
    return (rotated, coupling)
```

```python
import jax
import jax.numpy as jnp
from jax import lax
from jax.experimental import pallas as pl
from jax.experimental.pallas import tpu as pltpu
from jax.sharding import Mesh
from jax.sharding import PartitionSpec as P

HI=lax.Precision.HIGHEST
F32=jnp.float32
N=512; T=128
def dot(a,b,ca,cb):
    return lax.dot_general(a,b,(((ca,),(cb,)),((),())),precision=HI,preferred_element_type=F32)
def spread(x): return jnp.broadcast_to(x,(8,T))
def leaves(mats, B=4):
    sub=lax.broadcasted_iota(jnp.int32,(8,T),0); lane=lax.broadcasted_iota(jnp.int32,(8,T),1)
    n=len(mats); G8=T//8
    As=[list(m) for m in mats]
    Is=[[jnp.where(sub+8*q==lane,1.0,0.0).astype(F32) for q in range(G8)] for _ in range(n)]
    for P in range(0,G8,B):
        for p in range(P,P+B):
            r0=8*p
            qs=list(range(p,P+B))
            C=[{q:[spread(A[q][:,r0+k:r0+k+1]) for k in range(8)] for q in qs} for A in As]
            rd=[jnp.ones((8,T),F32) for _ in range(n)]
            for j in range(8):
                for a in range(n):
                    A,I=As[a],Is[a]
                    rinv=1.0/spread(C[a][p][j][j:j+1,:])
                    rd[a]=jnp.where(sub==j,rinv,rd[a])
                    rows=[spread(C[a][p][k][j:j+1,:]) for k in range(j+1,8)]
                    ra=spread(A[p][j:j+1,:]); ri=spread(I[p][j:j+1,:])
                    for q in qs:
                        if q==p:
                            if j==7: continue
                            m=jnp.where(sub>j,C[a][q][j]*rinv,0.0)
                        else:
                            m=C[a][q][j]*rinv
                        for k in range(j+1,8):
                            C[a][q][k]=C[a][q][k]-m*rows[k-j-1]
                        A[q]=A[q]-m*ra; I[q]=I[q]-m*ri
            for a in range(n):
                s=jnp.sqrt(rd[a])
                As[a][p]=As[a][p]*s; Is[a][p]=Is[a][p]*s
        if P+B<G8:
            for a in range(n):
                A,I=As[a],Is[a]
                SA=jnp.concatenate(A[P:P+B],axis=0)
                both=jnp.concatenate([SA,jnp.concatenate(I[P:P+B],axis=0)],axis=1)
                upd=dot(SA[:,8*(P+B):],both,0,0)
                for q in range(P+B,G8):
                    o=8*(q-P-B)
                    A[q]=A[q]-upd[o:o+8,:T]; I[q]=I[q]-upd[o:o+8,T:]
    for a in range(n):
        for p in range(G8):
            As[a][p]=jnp.where(lane>=sub+8*p,As[a][p],0.0)
    return As,Is
def kern(g_ref,pair_ref,turned_ref,top_ref,bot_ref,cpl_ref,A,U,V,W,Bc,RT,d_ref,u_ref,i_ref):
    A[...]=g_ref[...]
    H=N//2
    eye=lax.broadcasted_iota(jnp.int32,(H,H),0)==lax.broadcasted_iota(jnp.int32,(H,H),1)
    dt=jnp.sum(jnp.where(eye,g_ref[:H,:H],0.0),axis=1,keepdims=True)
    db=jnp.sum(jnp.where(eye,g_ref[H:,H:],0.0),axis=0,keepdims=True)
    cr=g_ref[:H,H:]
    cpl_ref[...]=jnp.broadcast_to(jnp.sum(jnp.sum(cr*cr/(dt*db),axis=0,keepdims=True),axis=1,keepdims=True),(8,T))
    U[...]=jnp.zeros_like(U); V[...]=jnp.zeros_like(V)
    d_ref[0]=g_ref[:T,:T]
    sub=lax.broadcasted_iota(jnp.int32,(T,T),0); lane=lax.broadcasted_iota(jnp.int32,(T,T),1)
    d_ref[1]=jnp.where(sub==lane,1.0,0.0).astype(F32)
    def branch(t):
        lo,hi=t*T,(t+1)*T
        if t>=1:
            s=t-1; sl,sh=s*T,t*T
            V[sl:sh,sl:sh]=u_ref[1]
            sinv=i_ref[1]
            W[sl:sh,sl:sh]=sinv
            if s:
                t1=dot(V[:sl,sl:sh],W[:sl,:sl],0,0)
                W[sl:sh,:sl]=-dot(sinv,t1,1,0)
                W[:sl,sl:sh]=jnp.zeros((sl,T),F32)
        if t<4:
            U[lo:hi,lo:hi]=u_ref[0]
            linv=i_ref[0]
            if t<3:
                U[lo:hi,hi:]=dot(linv,A[lo:hi,hi:],1,0)
                d_ref[0]=A[hi:hi+T,hi:hi+T]-dot(U[lo:hi,hi:hi+T],U[lo:hi,hi:hi+T],0,0)
            bcol=dot(U[:hi,lo:],U[lo:hi,lo:],1,1)
            if t:
                vcol=dot(W[:lo,:lo],bcol[:lo],1,0)
                V[:lo,lo:hi]=vcol
                d_ref[1]=bcol[lo:]-dot(vcol,vcol,0,0)
            else:
                d_ref[1]=bcol
            for i in range(t+1,4):
                a,b=i*T,(i+1)*T
                A[a:b,a:]=A[a:b,a:]-dot(U[lo:hi,a:b],U[lo:hi,a:],0,0)
        if t>=1:
            RT[sl:sh,:]=dot(W[sl:sh,:sh],U[:sh,:],1,0)
    def stage(t,c):
        us,is_=leaves([[d_ref[a,8*q:8*q+8,:] for q in range(T//8)] for a in range(2)])
        for a in range(2):
            for q in range(T//8):
                u_ref[a,8*q:8*q+8,:]=us[a][q]; i_ref[a,8*q:8*q+8,:]=is_[a][q]
        for k in range(5):
            pl.when(t==k)(lambda k=k: branch(k))
        return c
    lax.fori_loop(0,5,stage,0)
    turned_ref[...]=dot(pair_ref[...],RT[...],1,1)
    top_ref[...]=dot(V[:256,:],V[:256,:],1,1)
    bot_ref[...]=dot(V[256:,256:],V[256:,256:],1,1)
def step(g,pair):
    vm=pl.BlockSpec(memory_space=pltpu.VMEM)
    return pl.pallas_call(kern,out_shape=[jax.ShapeDtypeStruct((256,512),F32),jax.ShapeDtypeStruct((256,256),F32),jax.ShapeDtypeStruct((256,256),F32),jax.ShapeDtypeStruct((8,T),F32)],
        in_specs=[vm,vm],out_specs=[vm]*4,
        scratch_shapes=[pltpu.VMEM((N,N),F32)]*4+[pltpu.VMEM((N,T),F32),pltpu.VMEM((N,N),F32)]+[pltpu.VMEM((2,T,T),F32)]*3,
        name="rotate")(g,pair)

STEPS = 2
ROW = ("row_0", "row_1", "row_2")


def padded_to(lines, count):
    spare = -len(lines) % count
    return jnp.pad(lines, [(0, spare)] + [(0, 0)] * (lines.ndim - 1))


def copy_for_each(value, axis):
    copies = jnp.broadcast_to(value, (lax.axis_size(axis), *value.shape))
    return lax.all_to_all(copies, axis, split_axis=0, concat_axis=0, tiled=True)


def in_order(parts, dim):
    parts = jnp.moveaxis(parts, 0, dim)
    shape = parts.shape
    return parts.reshape(*shape[:dim], shape[dim] * shape[dim + 1], *shape[dim + 2 :])


def gather_axes(value, axes, dim):
    far, near = axes
    parts = copy_for_each(copy_for_each(value, far), near)
    return in_order(parts.swapaxes(0, 1).reshape(-1, *value.shape), dim)


def cut_along(value, dim, count):
    before, after = (value.shape[:dim], value.shape[dim + 1 :])
    return jnp.moveaxis(value.reshape(*before, count, -1, *after), dim, 0)


def summed_on_arrival(value, axis, dim):
    count = lax.axis_size(axis)
    parts = lax.all_to_all(cut_along(value, dim, count), axis, 0, 0, tiled=True)
    return jnp.sum(parts, axis=0)


def sum_in_two_steps(value, axes, dim):
    far, near = axes
    own = summed_on_arrival(cut_along(value, dim, lax.axis_size(far)), near, dim + 1)
    return jnp.sum(lax.all_to_all(own, far, 0, 0, tiled=True), axis=0)


def total_of(value, axes):
    lines = value.reshape(-1, value.shape[-1])
    padded = padded_to(lines, lax.axis_size(axes[0]) * lax.axis_size(axes[1]))
    whole = gather_axes(sum_in_two_steps(padded, axes, 0), axes, 0)
    return lax.slice_in_dim(whole, 0, len(lines)).reshape(value.shape)


def from_behind(value, axis, steps):
    count = lax.axis_size(axis)
    first, last = (max(0, -steps), min(count, count - steps))
    return lax.ppermute(value, axis, [(source, source + steps) for source in range(first, last)])


def gathered_copies(value, axis, dim):
    return in_order(copy_for_each(value, axis), dim)


def nested_sum(value, axes):
    lines = value.reshape(-1, value.shape[-1])
    own = summed_on_arrival(padded_to(lines, lax.axis_size(axes)), axes, 0)
    whole = gathered_copies(own, axes, 0)
    return whole[: len(lines)].reshape(value.shape)


def over_copies(value, axis):
    return copy_for_each(value, axis).sum(axis=0)


def pair_grams(pair_blocks):
    return jnp.einsum(
        "prk,prl->pkl",
        pair_blocks,
        pair_blocks,
        precision=lax.Precision.HIGHEST,
        preferred_element_type=jnp.float32,
    )


def body(matrix):
    row_total = matrix.shape[0]
    width = matrix.shape[1] // 2
    col_place = lax.axis_index("col")
    col_last = lax.axis_size("col") - 1
    first_col = col_place == 0
    last_col = col_place == col_last
    top_block = matrix[:, :width]
    bottom_block = matrix[:, width:]
    pair_blocks = matrix[None]
    pair_gram = total_of(pair_grams(pair_blocks), (("row_0", "row_1"), "row_2"))
    coupling_terms = []
    for step_index in range(STEPS):
        turned, own_top, own_bottom, term = step(pair_gram[0], pair_blocks[0])
        turned, own_top, own_bottom = turned[None], own_top[None], own_bottom[None]
        coupling_terms.append(term[0, 0])
        new_top = turned[0, :, :width]
        new_bottom = turned[0, :, width:]
        carried_top = jnp.concatenate([new_top, own_top[0]], axis=0)
        carried_bottom = jnp.concatenate([new_bottom, own_bottom[0]], axis=0)
        outgoing = jnp.where(first_col, carried_bottom, carried_top)
        arrived_top = from_behind(outgoing, "col", 1)
        arrived_bottom = from_behind(carried_bottom, "col", -1)
        top_whole = jnp.where(first_col, carried_top, arrived_top)
        bottom_whole = jnp.where(last_col, carried_top, arrived_bottom)
        top_block = top_whole[:row_total]
        bottom_block = bottom_whole[:row_total]
        pair_blocks = jnp.concatenate([top_block, bottom_block], axis=1)[None]
        if step_index + 1 < STEPS:
            cross_part = jnp.einsum(
                "prk,prl->pkl",
                top_block[None],
                bottom_block[None],
                precision=lax.Precision.HIGHEST,
                preferred_element_type=jnp.float32,
            )
            cross_total = nested_sum(cross_part, ROW)
            top_own = top_whole[row_total:][None]
            bottom_own = bottom_whole[row_total:][None]
            upper_half = jnp.concatenate([top_own, cross_total], axis=2)
            lower_half = jnp.concatenate([jnp.swapaxes(cross_total, 1, 2), bottom_own], axis=2)
            pair_gram = jnp.concatenate([upper_half, lower_half], axis=1)
    totals = over_copies(jnp.stack(coupling_terms), "col")
    coupling = jnp.sqrt(totals / (1.0 * lax.axis_size("col") * width))
    rotated = jnp.concatenate([top_block, bottom_block], axis=1)
    return (rotated, coupling)


def solution(mesh):
    split = Mesh(
        mesh.devices.reshape(8, 2, 2, mesh.shape["col"]), ("row_0", "row_1", "row_2", "col")
    )
    placed = (P(ROW, "col"),)
    return jax.shard_map(
        body, mesh=split, in_specs=placed, out_specs=(P(ROW, "col"), P()), check_vma=False
    )
```

```python
import functools

import jax
import jax.numpy as jnp
from jax import lax
from jax.experimental import pallas as pl
from jax.experimental.pallas import tpu as pltpu
from jax.sharding import Mesh
from jax.sharding import PartitionSpec as P

STEPS = 2
ROW = ("row_0", "row_1", "row_2")
CHIPS = ("row_0", "row_1")
H = 256
TOP = ((0, 0), (0, 1), (1, 1))
CROSS = ((0, 2), (0, 3), (1, 2), (1, 3))
BOTTOM = ((2, 2), (2, 3), (3, 3))
VM = pl.BlockSpec(memory_space=pltpu.VMEM)
SM = pl.BlockSpec(memory_space=pltpu.SMEM)

HI=lax.Precision.HIGHEST
F32=jnp.float32
N=512
T=128
def dot(a,b,ca,cb):
    return lax.dot_general(a,b,(((ca,),(cb,)),((),())),precision=HI,preferred_element_type=F32)
def spread(x): return jnp.broadcast_to(x,(8,T))
def leaves(mats, B=4):
    sub=lax.broadcasted_iota(jnp.int32,(8,T),0); lane=lax.broadcasted_iota(jnp.int32,(8,T),1)
    n=len(mats); G8=T//8
    As=[list(m) for m in mats]
    Is=[[jnp.where(sub+8*q==lane,1.0,0.0).astype(F32) for q in range(G8)] for _ in range(n)]
    for P in range(0,G8,B):
        for p in range(P,P+B):
            r0=8*p
            qs=list(range(p,P+B))
            C=[{q:[spread(A[q][:,r0+k:r0+k+1]) for k in range(8)] for q in qs} for A in As]
            rd=[jnp.ones((8,T),F32) for _ in range(n)]
            for j in range(8):
                for a in range(n):
                    A,I=As[a],Is[a]
                    rinv=1.0/spread(C[a][p][j][j:j+1,:])
                    rd[a]=jnp.where(sub==j,rinv,rd[a])
                    rows=[spread(C[a][p][k][j:j+1,:]) for k in range(j+1,8)]
                    ra=spread(A[p][j:j+1,:]); ri=spread(I[p][j:j+1,:])
                    for q in qs:
                        if q==p:
                            if j==7: continue
                            m=jnp.where(sub>j,C[a][q][j]*rinv,0.0)
                        else:
                            m=C[a][q][j]*rinv
                        for k in range(j+1,8):
                            C[a][q][k]=C[a][q][k]-m*rows[k-j-1]
                        A[q]=A[q]-m*ra; I[q]=I[q]-m*ri
            for a in range(n):
                s=jnp.sqrt(rd[a])
                As[a][p]=As[a][p]*s; Is[a][p]=Is[a][p]*s
        if P+B<G8:
            for a in range(n):
                A,I=As[a],Is[a]
                SA=jnp.concatenate(A[P:P+B],axis=0)
                both=jnp.concatenate([SA,jnp.concatenate(I[P:P+B],axis=0)],axis=1)
                upd=dot(SA[:,8*(P+B):],both,0,0)
                for q in range(P+B,G8):
                    o=8*(q-P-B)
                    A[q]=A[q]-upd[o:o+8,:T]; I[q]=I[q]-upd[o:o+8,T:]
    for a in range(n):
        for p in range(G8):
            As[a][p]=jnp.where(lane>=sub+8*p,As[a][p],0.0)
    return As,Is

def tile(ij):
    i,j=ij
    return slice(i*T,(i+1)*T),slice(j*T,(j+1)*T)
def gram_kernel(pair_ref,g_ref):
    where={ij:n for n,ij in enumerate(TOP+CROSS+BOTTOM)}
    for i in range(4):
        rows=dot(pair_ref[:,i*T:(i+1)*T],pair_ref[:,i*T:],0,0)
        for j in range(i,4):
            n=where[(i,j)]
            g_ref[n*T:(n+1)*T,:]=rows[:,(j-i)*T:(j-i+1)*T]
def local_gram(pair):
    return pl.pallas_call(gram_kernel,out_shape=jax.ShapeDtypeStruct((10*T,T),F32),in_specs=[VM],out_specs=VM,name="gram")(pair)
def cross_kernel(ends_ref,top_ref,from_left_ref,from_right_ref,pair_ref,c_ref):
    own=top_ref[...]
    top=jnp.where(ends_ref[0]==1,own,from_left_ref[...])
    bottom=jnp.where(ends_ref[1]==1,own,from_right_ref[...])
    pair_ref[:,:H]=top
    pair_ref[:,H:]=bottom
    for i in range(2):
        rows=dot(top[:,i*T:(i+1)*T],bottom,0,0)
        c_ref[2*i*T:(2*i+1)*T,:]=rows[:,:T]
        c_ref[(2*i+1)*T:(2*i+2)*T,:]=rows[:,T:]
def local_cross(ends,top,from_left,from_right):
    return pl.pallas_call(cross_kernel,out_shape=[jax.ShapeDtypeStruct((256,512),F32),jax.ShapeDtypeStruct((4*T,T),F32)],
        in_specs=[SM,VM,VM,VM],out_specs=[VM]*2,name="cross")(ends,top,from_left,from_right)
def diagonals(A,sub,lane):
    eye=sub==lane
    down=[jnp.sum(jnp.where(eye,A[tile((i,i))],0.0),axis=1,keepdims=True) for i in (0,1)]
    along=[jnp.sum(jnp.where(eye,A[tile((i,i))],0.0),axis=0,keepdims=True) for i in (2,3)]
    return down,along
def rotate_kernel(first,*refs):
    if first:
        ends_ref,g_ref,pair_ref,top_ref,bottom_ref,right_ref,own_top_ref,own_bottom_ref,own_right_ref,cpl_ref=refs[:10]
        refs=refs[10:]
    else:
        ends_ref,own_ref,own_left_ref,own_from_right_ref,g_ref,pair_ref,top_ref,bottom_ref,right_ref,cpl_ref=refs[:10]
        refs=refs[10:]
    A,U,V,W,RT,d_ref,u_ref,i_ref=refs
    sub=lax.broadcasted_iota(jnp.int32,(T,T),0); lane=lax.broadcasted_iota(jnp.int32,(T,T),1)
    if first:
        for n,ij in enumerate(TOP+CROSS+BOTTOM):
            A[tile(ij)]=g_ref[n*T:(n+1)*T,:]
    else:
        own=own_ref[...]
        own_top=jnp.where(ends_ref[0]==1,own,own_left_ref[...])
        own_bottom=jnp.where(ends_ref[1]==1,own,own_from_right_ref[...])
        for n in range(3):
            A[tile(TOP[n])]=own_top[n*T:(n+1)*T]
            A[tile(BOTTOM[n])]=own_bottom[n*T:(n+1)*T]
        for n,ij in enumerate(CROSS):
            A[tile(ij)]=g_ref[n*T:(n+1)*T,:]
    U[...]=jnp.zeros_like(U); V[...]=jnp.zeros_like(V)
    d_ref[0]=A[:T,:T]
    d_ref[1]=jnp.where(sub==lane,1.0,0.0).astype(F32)
    down,along=diagonals(A,sub,lane)
    cpl=jnp.zeros((1,T),F32)
    for i in (0,1):
        for j in (2,3):
            c=A[tile((i,j))]
            cpl=cpl+jnp.sum(c*c/(down[i]*along[j-2]),axis=0,keepdims=True)
    cpl_ref[...]=jnp.broadcast_to(jnp.sum(cpl,axis=1,keepdims=True),(8,T))
    def branch(t):
        lo,hi=t*T,(t+1)*T
        if t>=1:
            s=t-1; sl,sh=s*T,t*T
            V[sl:sh,sl:sh]=u_ref[1]
            sinv=i_ref[1]
            W[sl:sh,sl:sh]=sinv
            if s:
                t1=dot(V[:sl,sl:sh],W[:sl,:sl],0,0)
                W[sl:sh,:sl]=-dot(sinv,t1,1,0)
                W[:sl,sl:sh]=jnp.zeros((sl,T),F32)
        if t<4:
            U[lo:hi,lo:hi]=u_ref[0]
            linv=i_ref[0]
            if t<3:
                U[lo:hi,hi:]=dot(linv,A[lo:hi,hi:],1,0)
                d_ref[0]=A[hi:hi+T,hi:hi+T]-dot(U[lo:hi,hi:hi+T],U[lo:hi,hi:hi+T],0,0)
            bcol=dot(U[:hi,lo:],U[lo:hi,lo:],1,1)
            if t:
                vcol=dot(W[:lo,:lo],bcol[:lo],1,0)
                V[:lo,lo:hi]=vcol
                d_ref[1]=bcol[lo:]-dot(vcol,vcol,0,0)
            else:
                d_ref[1]=bcol
            for i in range(t+1,4):
                a,b=i*T,(i+1)*T
                A[a:b,a:]=A[a:b,a:]-dot(U[lo:hi,a:b],U[lo:hi,a:],0,0)
        if t>=1:
            RT[sl:sh,:]=dot(W[sl:sh,:sh],U[:sh,:],1,0)
    def stage(t,c):
        us,is_=leaves([[d_ref[a,8*q:8*q+8,:] for q in range(T//8)] for a in range(2)])
        for a in range(2):
            for q in range(T//8):
                u_ref[a,8*q:8*q+8,:]=us[a][q]; i_ref[a,8*q:8*q+8,:]=is_[a][q]
        for k in range(5):
            pl.when(t==k)(functools.partial(branch,k))
        return c
    lax.fori_loop(0,5,stage,0)
    turned=dot(pair_ref[...],RT[...],1,1)
    top,bottom=turned[:,:H],turned[:,H:]
    top_ref[...]=top
    bottom_ref[...]=bottom
    at_start=ends_ref[0]==1
    right_ref[...]=jnp.where(at_start,bottom,top)
    if first:
        def packed(ref,lo):
            a=dot(V[lo:lo+T,lo:],V[lo:lo+H,lo:],1,1)
            b=dot(V[lo+T:lo+H,lo:],V[lo+T:lo+H,lo:],1,1)
            ref[:T,:]=a[:,:T]
            ref[T:2*T,:]=a[:,T:]
            ref[2*T:,:]=b
        packed(own_top_ref,0)
        packed(own_bottom_ref,H)
        own_right_ref[...]=jnp.where(at_start,own_bottom_ref[...],own_top_ref[...])
def rotate(first,*operands):
    block=jax.ShapeDtypeStruct((256,H),F32)
    own=jax.ShapeDtypeStruct((3*T,T),F32)
    outs=[block]*3+([own]*3 if first else [])+[jax.ShapeDtypeStruct((8,T),F32)]
    return pl.pallas_call(functools.partial(rotate_kernel,first),out_shape=outs,
        in_specs=[SM]+[VM]*(len(operands)-1),out_specs=[VM]*len(outs),
        scratch_shapes=[pltpu.VMEM((N,N),F32)]*5+[pltpu.VMEM((2,T,T),F32)]*3,
        cost_estimate=pl.CostEstimate(flops=4_000_000_000,bytes_accessed=2_000_000,transcendentals=0),
        name="rotate")(*operands)


def scattered_sum(value, axis):
    count = lax.axis_size(axis)
    parts = lax.all_to_all(value.reshape(count, -1, T), axis, 0, 0, tiled=True)
    return jnp.sum(parts, axis=0)


def gathered(value, axis):
    copies = jnp.broadcast_to(value, (lax.axis_size(axis), *value.shape))
    return lax.all_to_all(copies, axis, split_axis=0, concat_axis=0, tiled=True).reshape(-1, T)


def row_total(value):
    own = scattered_sum(scattered_sum(value, "row_2"), CHIPS)
    return gathered(gathered(own, CHIPS), "row_2")


def moved(value, steps):
    count = lax.axis_size("col")
    first, last = max(0, -steps), min(count, count - steps)
    return lax.ppermute(value, "col", [(source, source + steps) for source in range(first, last)])


def over_slots(terms):
    count = lax.axis_size("col")
    own = jnp.where(jnp.arange(count)[:, None] == lax.axis_index("col"), terms, 0.0)
    parts = [own]
    for step in range(1, count):
        parts.append(lax.ppermute(own, "col", [(i, (i + step) % count) for i in range(count)]))
    return jnp.sum(sum(parts[1:], parts[0]), axis=0)


def steps(matrix):
    place = lax.axis_index("col")
    at_start = place == 0
    at_end = place == lax.axis_size("col") - 1
    ends = jnp.stack([at_start, at_end]).astype(jnp.int32)
    total = row_total(local_gram(matrix))
    top, bottom, right, own_top, own_bottom, own_right, term_0 = rotate(True, ends, total, matrix)
    from_left, from_right = moved(right, 1), moved(bottom, -1)
    pair, cross = local_cross(ends, top, from_left, from_right)
    own_right, own_away, cross = lax.optimization_barrier((own_right, own_bottom, cross))
    own_left = moved(own_right, 1)
    own_from_right = moved(own_away, -1)
    cross = scattered_sum(cross, "row_2")
    cross = gathered(gathered(scattered_sum(cross, CHIPS), CHIPS), "row_2")
    top, bottom, right, term_1 = rotate(False, ends, own_top, own_left, own_from_right, cross, pair)
    from_left = moved(right, 1)
    from_right = moved(bottom, -1)
    lane = jnp.arange(T)[None, :]
    totals = over_slots(jnp.where(lane == 0, term_0, term_1))
    coupling = jnp.sqrt(totals[:STEPS] / (1.0 * lax.axis_size("col") * H))
    rotated = jnp.concatenate(
        [jnp.where(at_start, top, from_left), jnp.where(at_end, top, from_right)], axis=1
    )
    return (rotated, coupling)


def solution(mesh):
    split = Mesh(
        mesh.devices.reshape(8, 2, 2, mesh.shape["col"]), ("row_0", "row_1", "row_2", "col")
    )
    placed = (P(ROW, "col"),)
    return jax.shard_map(
        steps, mesh=split, in_specs=placed, out_specs=(P(ROW, "col"), P()), check_vma=False
    )
```

```python
import functools

import jax
import jax.numpy as jnp
from jax import lax
from jax.experimental import pallas as pl
from jax.experimental.pallas import tpu as pltpu
from jax.sharding import Mesh
from jax.sharding import PartitionSpec as P

ROW = ("row_0", "row_1", "row_2")
CHIPS = ("row_0", "row_1")
H = 256
TOP = ((0, 0), (0, 1), (1, 1))
CROSS = ((0, 2), (0, 3), (1, 2), (1, 3))
BOTTOM = ((2, 2), (2, 3), (3, 3))
VM = pl.BlockSpec(memory_space=pltpu.VMEM)
SM = pl.BlockSpec(memory_space=pltpu.SMEM)

HI=lax.Precision.HIGHEST
F32=jnp.float32
N=512
T=128
def dot(a,b,ca,cb):
    return lax.dot_general(a,b,(((ca,),(cb,)),((),())),precision=HI,preferred_element_type=F32)
def spread(x): return jnp.broadcast_to(x,(8,T))
def leaves(mats, B=4):
    sub=lax.broadcasted_iota(jnp.int32,(8,T),0); lane=lax.broadcasted_iota(jnp.int32,(8,T),1)
    n=len(mats); G8=T//8
    As=[list(m) for m in mats]
    Is=[[jnp.where(sub+8*q==lane,1.0,0.0).astype(F32) for q in range(G8)] for _ in range(n)]
    for P in range(0,G8,B):
        for p in range(P,P+B):
            r0=8*p
            qs=list(range(p,P+B))
            C=[{q:[spread(A[q][:,r0+k:r0+k+1]) for k in range(8)] for q in qs} for A in As]
            rd=[jnp.ones((8,T),F32) for _ in range(n)]
            for j in range(8):
                for a in range(n):
                    A,I=As[a],Is[a]
                    rinv=1.0/spread(C[a][p][j][j:j+1,:])
                    rd[a]=jnp.where(sub==j,rinv,rd[a])
                    rows=[spread(C[a][p][k][j:j+1,:]) for k in range(j+1,8)]
                    ra=spread(A[p][j:j+1,:]); ri=spread(I[p][j:j+1,:])
                    for q in qs:
                        if q==p:
                            if j==7: continue
                            cm=jnp.where(sub>j,C[a][q][j],0.0)
                            for k in range(j+1,8):
                                C[a][q][k]=C[a][q][k]-(cm*rows[k-j-1])*rinv
                            m=cm*rinv
                        else:
                            m=C[a][q][j]*rinv
                            for k in range(j+1,8):
                                C[a][q][k]=C[a][q][k]-m*rows[k-j-1]
                        A[q]=A[q]-m*ra; I[q]=I[q]-m*ri
            for a in range(n):
                s=jnp.sqrt(rd[a])
                As[a][p]=As[a][p]*s; Is[a][p]=Is[a][p]*s
        if P+B<G8:
            for a in range(n):
                A,I=As[a],Is[a]
                SA=jnp.concatenate(A[P:P+B],axis=0)
                both=jnp.concatenate([SA,jnp.concatenate(I[P:P+B],axis=0)],axis=1)
                upd=dot(SA[:,8*(P+B):],both,0,0)
                for q in range(P+B,G8):
                    o=8*(q-P-B)
                    A[q]=A[q]-upd[o:o+8,:T]; I[q]=I[q]-upd[o:o+8,T:]
    for a in range(n):
        for p in range(G8):
            As[a][p]=jnp.where(lane>=sub+8*p,As[a][p],0.0)
    return As,Is

def tile(ij):
    i,j=ij
    return slice(i*T,(i+1)*T),slice(j*T,(j+1)*T)
def gram_kernel(pair_ref,g_ref):
    where={ij:n for n,ij in enumerate(TOP+CROSS+BOTTOM)}
    for i in range(4):
        rows=dot(pair_ref[:,i*T:(i+1)*T],pair_ref[:,i*T:],0,0)
        for j in range(i,4):
            n=where[(i,j)]
            g_ref[n*T:(n+1)*T,:]=rows[:,(j-i)*T:(j-i+1)*T]
def local_gram(pair):
    return pl.pallas_call(gram_kernel,out_shape=jax.ShapeDtypeStruct((10*T,T),F32),in_specs=[VM],out_specs=VM,name="gram")(pair)
def cross_kernel(ends_ref,top_ref,from_left_ref,from_right_ref,pair_ref,c_ref):
    own=top_ref[...]
    top=jnp.where(ends_ref[0]==1,own,from_left_ref[...])
    bottom=jnp.where(ends_ref[1]==1,own,from_right_ref[...])
    pair_ref[:,:H]=top
    pair_ref[:,H:]=bottom
    for i in range(2):
        rows=dot(top[:,i*T:(i+1)*T],bottom,0,0)
        c_ref[2*i*T:(2*i+1)*T,:]=rows[:,:T]
        c_ref[(2*i+1)*T:(2*i+2)*T,:]=rows[:,T:]
def local_cross(ends,top,from_left,from_right):
    return pl.pallas_call(cross_kernel,out_shape=[jax.ShapeDtypeStruct((256,512),F32),jax.ShapeDtypeStruct((4*T,T),F32)],
        in_specs=[SM,VM,VM,VM],out_specs=[VM]*2,name="cross")(ends,top,from_left,from_right)
def spread_leaves(d_ref,u_ref,i_ref,count):
    us,is_=leaves([[d_ref[a,8*q:8*q+8,:] for q in range(T//8)] for a in range(count)])
    for a in range(count):
        for q in range(T//8):
            u_ref[a,8*q:8*q+8,:]=us[a][q]
            i_ref[a,8*q:8*q+8,:]=is_[a][q]
def early_kernel(ends_ref,own_ref,own_left_ref,up_ref,inv_ref,d_ref,u_ref,i_ref):
    g=jnp.where(ends_ref[0]==1,own_ref[...],own_left_ref[...])
    d_ref[0]=g[:T]
    up_ref[T:2*T,:]=g[T:2*T]
    inv_ref[T:2*T,:]=g[2*T:]
    def stage(t,c):
        spread_leaves(d_ref,u_ref,i_ref,1)
        @pl.when(t==0)
        def _():
            up_ref[:T,:]=u_ref[0]
            inv_ref[:T,:]=i_ref[0]
            u01=dot(i_ref[0],up_ref[T:2*T,:],1,0)
            up_ref[T:2*T,:]=u01
            d_ref[0]=inv_ref[T:2*T,:]-dot(u01,u01,0,0)
        @pl.when(t==1)
        def _():
            up_ref[2*T:,:]=u_ref[0]
            inv_ref[2*T:,:]=i_ref[0]
            inv_ref[T:2*T,:]=-dot(i_ref[0],dot(up_ref[T:2*T,:],inv_ref[:T,:],0,0),1,0)
        return c
    lax.fori_loop(0,2,stage,0)
def early(*operands):
    own=jax.ShapeDtypeStruct((3*T,T),F32)
    return pl.pallas_call(early_kernel,out_shape=[own]*2,in_specs=[SM,VM,VM],out_specs=[VM]*2,
        scratch_shapes=[pltpu.VMEM((1,T,T),F32)]*3,
        cost_estimate=pl.CostEstimate(flops=500_000_000,bytes_accessed=1_000_000,transcendentals=0),
        name="early")(*operands)
def coupling_sum(A,down,along):
    cpl=jnp.zeros((1,T),F32)
    for i in (0,1):
        for j in (2,3):
            c=A[tile((i,j))]
            cpl=cpl+jnp.sum(c*c/(down[i]*along[j-2]),axis=0,keepdims=True)
    return jnp.broadcast_to(jnp.sum(cpl,axis=1,keepdims=True),(8,T))
def rotate_kernel(first,*refs):
    if first:
        ends_ref,g_ref,pair_ref,top_ref,bottom_ref,right_ref,own_top_ref,own_bottom_ref,own_right_ref,cpl_ref=refs[:10]
        refs=refs[10:]
    else:
        ends_ref,own_ref,own_from_right_ref,up_ref,inv_ref,g_ref,pair_ref,top_ref,bottom_ref,right_ref,cpl_ref=refs[:11]
        refs=refs[11:]
    A,U,V,W,RT,d_ref,u_ref,i_ref=refs
    sub=lax.broadcasted_iota(jnp.int32,(T,T),0); lane=lax.broadcasted_iota(jnp.int32,(T,T),1)
    eye=sub==lane
    U[...]=jnp.zeros_like(U); V[...]=jnp.zeros_like(V)
    def along_of(n):
        return jnp.sum(jnp.where(eye,A[tile((n,n))],0.0),axis=0,keepdims=True)
    def down_of(row):
        return jnp.sum(jnp.where(eye,row,0.0),axis=1,keepdims=True)
    def next_d2(t):
        lo,hi=t*T,(t+1)*T
        bcol=dot(U[:hi,lo:],U[lo:hi,lo:],1,1)
        if t:
            vcol=dot(W[:lo,:lo],bcol[:lo],1,0)
            V[:lo,lo:hi]=vcol
            d_ref[1]=bcol[lo:]-dot(vcol,vcol,0,0)
        else:
            d_ref[1]=bcol
    def inner_part(s):
        sl,sh=s*T,(s+1)*T
        V[sl:sh,sl:sh]=u_ref[1]
        sinv=i_ref[1]
        W[sl:sh,sl:sh]=sinv
        if s:
            t1=dot(V[:sl,sl:sh],W[:sl,:sl],0,0)
            W[sl:sh,:sl]=-dot(sinv,t1,1,0)
            W[:sl,sl:sh]=jnp.zeros((sl,T),F32)
    def outer_part(t):
        lo,hi=t*T,(t+1)*T
        U[lo:hi,lo:hi]=u_ref[0]
        if t<3:
            U[lo:hi,hi:]=dot(i_ref[0],A[lo:hi,hi:],1,0)
            d_ref[0]=A[hi:hi+T,hi:hi+T]-dot(U[lo:hi,hi:hi+T],U[lo:hi,hi:hi+T],0,0)
    def trailing(t):
        lo,hi=t*T,(t+1)*T
        for i in range(t+1,4):
            a,b=i*T,(i+1)*T
            A[a:b,a:]=A[a:b,a:]-dot(U[lo:hi,a:b],U[lo:hi,a:],0,0)
    def turn_row(s):
        sl,sh=s*T,(s+1)*T
        RT[sl:sh,:]=dot(W[sl:sh,:sh],U[:sh,:],1,0)
    if first:
        for n,ij in enumerate(TOP+CROSS+BOTTOM):
            A[tile(ij)]=g_ref[n*T:(n+1)*T,:]
        d_ref[0]=A[:T,:T]
        d_ref[1]=jnp.where(eye,1.0,0.0).astype(F32)
        down=[down_of(A[tile((n,n))]) for n in (0,1)]
        skip=0
    else:
        own_bottom=jnp.where(ends_ref[1]==1,own_ref[...],own_from_right_ref[...])
        for n in range(3):
            A[tile(BOTTOM[n])]=own_bottom[n*T:(n+1)*T]
            U[tile(TOP[n])]=up_ref[n*T:(n+1)*T,:]
        for n,ij in enumerate(CROSS):
            A[tile(ij)]=g_ref[n*T:(n+1)*T,:]
        sq=[jnp.sum(up_ref[n*T:(n+1)*T,:]*up_ref[n*T:(n+1)*T,:],axis=0,keepdims=True) for n in range(3)]
        down=[down_of(sq[0]),down_of(sq[1]+sq[2])]
        skip=2
    cpl_ref[...]=coupling_sum(A,down,[along_of(2),along_of(3)])
    if not first:
        U[:T,H:]=dot(inv_ref[:T,:],A[:T,H:],1,0)
        U[T:H,H:]=dot(inv_ref[T:2*T,:],A[:T,H:],1,0)+dot(inv_ref[2*T:,:],A[T:H,H:],1,0)
        for a in (H,H+T):
            A[a:a+T,a:]=A[a:a+T,a:]-dot(U[:H,a:a+T],U[:H,a:],0,0)
        d_ref[0]=A[H:H+T,H:H+T]
        next_d2(0)
    def branch(k):
        s=k-1 if first else k
        t=k+skip
        if s>=0:
            inner_part(s)
        if t<4:
            outer_part(t)
        if s+1<4:
            next_d2(s+1)
        if t<4:
            trailing(t)
        if s>=0:
            turn_row(s)
    stages=5 if first else 4
    def stage(t,c):
        spread_leaves(d_ref,u_ref,i_ref,2)
        for k in range(stages):
            pl.when(t==k)(functools.partial(branch,k))
        return c
    lax.fori_loop(0,stages,stage,0)
    turned=dot(pair_ref[...],RT[...],1,1)
    top,bottom=turned[:,:H],turned[:,H:]
    top_ref[...]=top
    bottom_ref[...]=bottom
    at_start=ends_ref[0]==1
    right_ref[...]=jnp.where(at_start,bottom,top)
    if first:
        def packed(ref,lo):
            a=dot(V[lo:lo+T,lo:],V[lo:lo+H,lo:],1,1)
            b=dot(V[lo+T:lo+H,lo:],V[lo+T:lo+H,lo:],1,1)
            ref[:T,:]=a[:,:T]
            ref[T:2*T,:]=a[:,T:]
            ref[2*T:,:]=b
        packed(own_top_ref,0)
        packed(own_bottom_ref,H)
        own_right_ref[...]=jnp.where(at_start,own_bottom_ref[...],own_top_ref[...])
def rotate(first,*operands):
    block=jax.ShapeDtypeStruct((256,H),F32)
    own=jax.ShapeDtypeStruct((3*T,T),F32)
    outs=[block]*3+([own]*3 if first else [])+[jax.ShapeDtypeStruct((8,T),F32)]
    return pl.pallas_call(functools.partial(rotate_kernel,first),out_shape=outs,
        in_specs=[SM]+[VM]*(len(operands)-1),out_specs=[VM]*len(outs),
        scratch_shapes=[pltpu.VMEM((N,N),F32)]*5+[pltpu.VMEM((2,T,T),F32)]*3,
        cost_estimate=pl.CostEstimate(flops=4_000_000_000,bytes_accessed=2_000_000,transcendentals=0),
        name="rotate")(*operands)


def scattered_sum(value, axis):
    count = lax.axis_size(axis)
    parts = lax.all_to_all(value.reshape(count, -1, T), axis, 0, 0, tiled=True)
    return jnp.sum(parts, axis=0)


def gathered(value, axis):
    copies = jnp.broadcast_to(value, (lax.axis_size(axis), *value.shape))
    return lax.all_to_all(copies, axis, split_axis=0, concat_axis=0, tiled=True).reshape(-1, T)


def row_total(value):
    own = scattered_sum(scattered_sum(value, "row_2"), CHIPS)
    return gathered(gathered(own, CHIPS), "row_2")


def moved(value, steps):
    count = lax.axis_size("col")
    first, last = max(0, -steps), min(count, count - steps)
    return lax.ppermute(value, "col", [(source, source + steps) for source in range(first, last)])


def over_slots(terms):
    copies = jnp.broadcast_to(terms, (lax.axis_size("col"), *terms.shape))
    return jnp.sum(lax.all_to_all(copies, "col", split_axis=0, concat_axis=0, tiled=True), axis=0)


def steps(matrix):
    place = lax.axis_index("col")
    at_start = place == 0
    at_end = place == lax.axis_size("col") - 1
    ends = jnp.stack([at_start, at_end]).astype(jnp.int32)
    total = row_total(local_gram(matrix))
    top, bottom, right, own_top, own_bottom, own_right, term_0 = rotate(True, ends, total, matrix)
    from_left = moved(right, 1)
    from_right = moved(bottom, -1)
    own_left = moved(own_right, 1)
    own_from_right = moved(own_bottom, -1)
    pair, cross = local_cross(ends, top, from_left, from_right)
    cross = scattered_sum(cross, ROW)
    cross = gathered(cross, ROW)
    up, inverse = early(ends, own_top, own_left)
    top, bottom, right, term_1 = rotate(
        False, ends, own_top, own_from_right, up, inverse, cross, pair
    )
    from_left = moved(right, 1)
    from_right = moved(bottom, -1)
    totals = over_slots(jnp.stack([term_0[0, 0], term_1[0, 0]]))
    coupling = jnp.sqrt(totals / (1.0 * lax.axis_size("col") * H))
    rotated = jnp.concatenate(
        [jnp.where(at_start, top, from_left), jnp.where(at_end, top, from_right)], axis=1
    )
    return (rotated, coupling)


def solution(mesh):
    split = Mesh(
        mesh.devices.reshape(8, 2, 2, mesh.shape["col"]), ("row_0", "row_1", "row_2", "col")
    )
    placed = (P(ROW, "col"),)
    return jax.shard_map(steps, mesh=split, in_specs=placed, out_specs=(P(ROW, "col"), P()), check_vma=False)
```

```python
import functools

import jax
import jax.numpy as jnp
from jax import lax
from jax.experimental import pallas as pl
from jax.experimental.pallas import tpu as pltpu
from jax.sharding import Mesh
from jax.sharding import PartitionSpec as P

STEPS = 2
ROW = ("row_0", "row_1", "row_2")
CHIPS = ("row_0", "row_1")
H = 256
TOP = ((0, 0), (0, 1), (1, 1))
CROSS = ((0, 2), (0, 3), (1, 2), (1, 3))
BOTTOM = ((2, 2), (2, 3), (3, 3))
VM = pl.BlockSpec(memory_space=pltpu.VMEM)
SM = pl.BlockSpec(memory_space=pltpu.SMEM)

HI=lax.Precision.HIGHEST
F32=jnp.float32
N=512
T=128
def dot(a,b,ca,cb):
    return lax.dot_general(a,b,(((ca,),(cb,)),((),())),precision=HI,preferred_element_type=F32)
def spread(x): return jnp.broadcast_to(x,(8,T))
def leaves(mats, B=4):
    sub=lax.broadcasted_iota(jnp.int32,(8,T),0); lane=lax.broadcasted_iota(jnp.int32,(8,T),1)
    n=len(mats); G8=T//8
    As=[list(m) for m in mats]
    Is=[[jnp.where(sub+8*q==lane,1.0,0.0).astype(F32) for q in range(G8)] for _ in range(n)]
    for P in range(0,G8,B):
        for p in range(P,P+B):
            r0=8*p
            qs=list(range(p,P+B))
            C=[{q:[spread(A[q][:,r0+k:r0+k+1]) for k in range(8)] for q in qs} for A in As]
            rd=[jnp.ones((8,T),F32) for _ in range(n)]
            for j in range(8):
                for a in range(n):
                    A,I=As[a],Is[a]
                    rinv=1.0/spread(C[a][p][j][j:j+1,:])
                    rd[a]=jnp.where(sub==j,rinv,rd[a])
                    rows=[spread(C[a][p][k][j:j+1,:]) for k in range(j+1,8)]
                    ra=spread(A[p][j:j+1,:]); ri=spread(I[p][j:j+1,:])
                    for q in qs:
                        if q==p:
                            if j==7: continue
                            cm=jnp.where(sub>j,C[a][q][j],0.0)
                            for k in range(j+1,8):
                                C[a][q][k]=C[a][q][k]-(cm*rows[k-j-1])*rinv
                            m=cm*rinv
                        else:
                            m=C[a][q][j]*rinv
                            for k in range(j+1,8):
                                C[a][q][k]=C[a][q][k]-m*rows[k-j-1]
                        A[q]=A[q]-m*ra; I[q]=I[q]-m*ri
            for a in range(n):
                s=jnp.sqrt(rd[a])
                As[a][p]=As[a][p]*s; Is[a][p]=Is[a][p]*s
        if P+B<G8:
            for a in range(n):
                A,I=As[a],Is[a]
                SA=jnp.concatenate(A[P:P+B],axis=0)
                both=jnp.concatenate([SA,jnp.concatenate(I[P:P+B],axis=0)],axis=1)
                upd=dot(SA[:,8*(P+B):],both,0,0)
                for q in range(P+B,G8):
                    o=8*(q-P-B)
                    A[q]=A[q]-upd[o:o+8,:T]; I[q]=I[q]-upd[o:o+8,T:]
    for a in range(n):
        for p in range(G8):
            As[a][p]=jnp.where(lane>=sub+8*p,As[a][p],0.0)
    return As,Is

def tile(ij):
    i,j=ij
    return slice(i*T,(i+1)*T),slice(j*T,(j+1)*T)
def gram_kernel(ends_ref,pair_ref,keep_ref,give_ref,g_ref):
    where={ij:n for n,ij in enumerate(TOP+CROSS+BOTTOM)}
    for i in range(4):
        rows=dot(pair_ref[:,i*T:(i+1)*T],pair_ref[:,i*T:],0,0)
        for j in range(i,4):
            n=where[(i,j)]
            g_ref[n*T:(n+1)*T,:]=rows[:,(j-i)*T:(j-i+1)*T]
    core=ends_ref[2]
    keep_ref[...]=g_ref[pl.ds(pl.multiple_of(core*(5*T),T),5*T),:]
    give_ref[...]=g_ref[pl.ds(pl.multiple_of((1-core)*(5*T),T),5*T),:]
def local_gram(ends,pair):
    half=jax.ShapeDtypeStruct((5*T,T),F32)
    return pl.pallas_call(gram_kernel,out_shape=[half]*2,in_specs=[SM,VM],out_specs=[VM]*2,
        scratch_shapes=[pltpu.VMEM((10*T,T),F32)],name="gram")(ends,pair)
def place_kernel(ends_ref,own_ref,from_left_ref,from_right_ref,o_ref):
    own=own_ref[...]
    o_ref[:,:H]=jnp.where(ends_ref[0]==1,own,from_left_ref[...])
    o_ref[:,H:]=jnp.where(ends_ref[1]==1,own,from_right_ref[...])
def placed_blocks(*operands):
    return pl.pallas_call(place_kernel,out_shape=jax.ShapeDtypeStruct((256,512),F32),in_specs=[SM]+[VM]*3,out_specs=VM,name="place")(*operands)
def cross_kernel(ends_ref,top_ref,from_left_ref,from_right_ref,pair_ref,c_ref):
    own=top_ref[...]
    top=jnp.where(ends_ref[0]==1,own,from_left_ref[...])
    bottom=jnp.where(ends_ref[1]==1,own,from_right_ref[...])
    pair_ref[:,:H]=top
    pair_ref[:,H:]=bottom
    for i in range(2):
        rows=dot(top[:,i*T:(i+1)*T],bottom,0,0)
        c_ref[2*i*T:(2*i+1)*T,:]=rows[:,:T]
        c_ref[(2*i+1)*T:(2*i+2)*T,:]=rows[:,T:]
def local_cross(ends,top,from_left,from_right):
    return pl.pallas_call(cross_kernel,out_shape=[jax.ShapeDtypeStruct((256,512),F32),jax.ShapeDtypeStruct((4*T,T),F32)],
        in_specs=[SM,VM,VM,VM],out_specs=[VM]*2,name="cross")(ends,top,from_left,from_right)
def spread_leaves(d_ref,u_ref,i_ref,count):
    us,is_=leaves([[d_ref[a,8*q:8*q+8,:] for q in range(T//8)] for a in range(count)])
    for a in range(count):
        for q in range(T//8):
            u_ref[a,8*q:8*q+8,:]=us[a][q]
            i_ref[a,8*q:8*q+8,:]=is_[a][q]
def early_kernel(ends_ref,own_ref,own_left_ref,up_ref,inv_ref,d_ref,u_ref,i_ref):
    g=jnp.where(ends_ref[0]==1,own_ref[...],own_left_ref[...])
    d_ref[0]=g[:T]
    up_ref[T:2*T,:]=g[T:2*T]
    inv_ref[T:2*T,:]=g[2*T:]
    def stage(t,c):
        spread_leaves(d_ref,u_ref,i_ref,1)
        @pl.when(t==0)
        def _():
            up_ref[:T,:]=u_ref[0]
            inv_ref[:T,:]=i_ref[0]
            u01=dot(i_ref[0],up_ref[T:2*T,:],1,0)
            up_ref[T:2*T,:]=u01
            d_ref[0]=inv_ref[T:2*T,:]-dot(u01,u01,0,0)
        @pl.when(t==1)
        def _():
            up_ref[2*T:,:]=u_ref[0]
            inv_ref[2*T:,:]=i_ref[0]
            inv_ref[T:2*T,:]=-dot(i_ref[0],dot(up_ref[T:2*T,:],inv_ref[:T,:],0,0),1,0)
        return c
    lax.fori_loop(0,2,stage,0)
def early(*operands):
    own=jax.ShapeDtypeStruct((3*T,T),F32)
    return pl.pallas_call(early_kernel,out_shape=[own]*2,in_specs=[SM,VM,VM],out_specs=[VM]*2,
        scratch_shapes=[pltpu.VMEM((1,T,T),F32)]*3,
        cost_estimate=pl.CostEstimate(flops=500_000_000,bytes_accessed=1_000_000,transcendentals=0),
        name="early")(*operands)
def coupling_sum(A,down,along):
    cpl=jnp.zeros((1,T),F32)
    for i in (0,1):
        for j in (2,3):
            c=A[tile((i,j))]
            cpl=cpl+jnp.sum(c*c/(down[i]*along[j-2]),axis=0,keepdims=True)
    return jnp.broadcast_to(jnp.sum(cpl,axis=1,keepdims=True),(8,T))
def rotate_kernel(first,*refs):
    if first:
        ends_ref,half_ref,rest_ref,pair_ref,top_ref,bottom_ref,right_ref,own_top_ref,own_bottom_ref,own_right_ref,cpl_ref=refs[:11]
        refs=refs[11:]
    else:
        ends_ref,own_ref,own_from_right_ref,up_ref,inv_ref,g_ref,pair_ref,term_ref,top_ref,bottom_ref,right_ref,cpl_ref=refs[:12]
        refs=refs[12:]
    A,U,V,W,RT,d_ref,u_ref,i_ref=refs
    sub=lax.broadcasted_iota(jnp.int32,(T,T),0); lane=lax.broadcasted_iota(jnp.int32,(T,T),1)
    eye=sub==lane
    U[...]=jnp.zeros_like(U); V[...]=jnp.zeros_like(V)
    def along_of(n):
        return jnp.sum(jnp.where(eye,A[tile((n,n))],0.0),axis=0,keepdims=True)
    def down_of(row):
        return jnp.sum(jnp.where(eye,row,0.0),axis=1,keepdims=True)
    def next_d2(t):
        lo,hi=t*T,(t+1)*T
        bcol=dot(U[:hi,lo:],U[lo:hi,lo:],1,1)
        if t:
            vcol=dot(W[:lo,:lo],bcol[:lo],1,0)
            V[:lo,lo:hi]=vcol
            d_ref[1]=bcol[lo:]-dot(vcol,vcol,0,0)
        else:
            d_ref[1]=bcol
    def inner_part(s):
        sl,sh=s*T,(s+1)*T
        V[sl:sh,sl:sh]=u_ref[1]
        sinv=i_ref[1]
        W[sl:sh,sl:sh]=sinv
        if s:
            t1=dot(V[:sl,sl:sh],W[:sl,:sl],0,0)
            W[sl:sh,:sl]=-dot(sinv,t1,1,0)
            W[:sl,sl:sh]=jnp.zeros((sl,T),F32)
    def outer_part(t):
        lo,hi=t*T,(t+1)*T
        U[lo:hi,lo:hi]=u_ref[0]
        if t<3:
            U[lo:hi,hi:]=dot(i_ref[0],A[lo:hi,hi:],1,0)
            d_ref[0]=A[hi:hi+T,hi:hi+T]-dot(U[lo:hi,hi:hi+T],U[lo:hi,hi:hi+T],0,0)
    def trailing(t):
        lo,hi=t*T,(t+1)*T
        for i in range(t+1,4):
            a,b=i*T,(i+1)*T
            A[a:b,a:]=A[a:b,a:]-dot(U[lo:hi,a:b],U[lo:hi,a:],0,0)
    def turn_row(s):
        sl,sh=s*T,(s+1)*T
        RT[sl:sh,:]=dot(W[sl:sh,:sh],U[:sh,:],1,0)
    if first:
        for n,ij in enumerate(TOP+CROSS+BOTTOM):
            m=(n%5)*T
            A[tile(ij)]=jnp.where(ends_ref[2]==n//5,half_ref[m:m+T,:],rest_ref[m:m+T,:])
        d_ref[0]=A[:T,:T]
        d_ref[1]=jnp.where(eye,1.0,0.0).astype(F32)
        down=[down_of(A[tile((n,n))]) for n in (0,1)]
        skip=0
    else:
        own_bottom=jnp.where(ends_ref[1]==1,own_ref[...],own_from_right_ref[...])
        for n in range(3):
            A[tile(BOTTOM[n])]=own_bottom[n*T:(n+1)*T]
            U[tile(TOP[n])]=up_ref[n*T:(n+1)*T,:]
        for n,ij in enumerate(CROSS):
            A[tile(ij)]=g_ref[n*T:(n+1)*T,:]
        sq=[jnp.sum(up_ref[n*T:(n+1)*T,:]*up_ref[n*T:(n+1)*T,:],axis=0,keepdims=True) for n in range(3)]
        down=[down_of(sq[0]),down_of(sq[1]+sq[2])]
        skip=2
    term=coupling_sum(A,down,[along_of(2),along_of(3)])
    if first:
        cpl_ref[...]=term
    else:
        cpl_ref[...]=jnp.where(lane[:8]==0,term_ref[...],term)
    if not first:
        U[:T,H:]=dot(inv_ref[:T,:],A[:T,H:],1,0)
        U[T:H,H:]=dot(inv_ref[T:2*T,:],A[:T,H:],1,0)+dot(inv_ref[2*T:,:],A[T:H,H:],1,0)
        for a in (H,H+T):
            A[a:a+T,a:]=A[a:a+T,a:]-dot(U[:H,a:a+T],U[:H,a:],0,0)
        d_ref[0]=A[H:H+T,H:H+T]
        next_d2(0)
    def branch(k):
        s=k-1 if first else k
        t=k+skip
        if s>=0:
            inner_part(s)
        if t<4:
            outer_part(t)
        if s+1<4:
            next_d2(s+1)
        if t<4:
            trailing(t)
        if s>=0:
            turn_row(s)
    stages=5 if first else 4
    def stage(t,c):
        spread_leaves(d_ref,u_ref,i_ref,2)
        for k in range(stages):
            pl.when(t==k)(functools.partial(branch,k))
        return c
    lax.fori_loop(0,stages,stage,0)
    turned=dot(pair_ref[...],RT[...],1,1)
    top,bottom=turned[:,:H],turned[:,H:]
    top_ref[...]=top
    bottom_ref[...]=bottom
    at_start=ends_ref[0]==1
    right_ref[...]=jnp.where(at_start,bottom,top)
    if first:
        def packed(ref,lo):
            a=dot(V[lo:lo+T,lo:],V[lo:lo+H,lo:],1,1)
            b=dot(V[lo+T:lo+H,lo:],V[lo+T:lo+H,lo:],1,1)
            ref[:T,:]=a[:,:T]
            ref[T:2*T,:]=a[:,T:]
            ref[2*T:,:]=b
        packed(own_top_ref,0)
        packed(own_bottom_ref,H)
        own_right_ref[...]=jnp.where(at_start,own_bottom_ref[...],own_top_ref[...])
def rotate(first,*operands):
    block=jax.ShapeDtypeStruct((256,H),F32)
    own=jax.ShapeDtypeStruct((3*T,T),F32)
    outs=[block]*3+([own]*3 if first else [])+[jax.ShapeDtypeStruct((8,T),F32)]
    return pl.pallas_call(functools.partial(rotate_kernel,first),out_shape=outs,
        in_specs=[SM]+[VM]*(len(operands)-1),out_specs=[VM]*len(outs),
        scratch_shapes=[pltpu.VMEM((N,N),F32)]*5+[pltpu.VMEM((2,T,T),F32)]*3,
        cost_estimate=pl.CostEstimate(flops=4_000_000_000,bytes_accessed=2_000_000,transcendentals=0),
        name="rotate")(*operands)


def scattered_sum(value, axis):
    count = lax.axis_size(axis)
    parts = lax.all_to_all(value.reshape(count, -1, T), axis, 0, 0, tiled=True)
    return jnp.sum(parts, axis=0)


def gathered(value, axis):
    copies = jnp.broadcast_to(value, (lax.axis_size(axis), *value.shape))
    return lax.all_to_all(copies, axis, split_axis=0, concat_axis=0, tiled=True).reshape(-1, T)


def swapped(value):
    return lax.ppermute(value, "row_2", [(0, 1), (1, 0)])


def row_halves(keep, give):
    half = gathered(scattered_sum(keep + swapped(give), CHIPS), CHIPS)
    return half, swapped(half)


def moved(value, steps):
    count = lax.axis_size("col")
    first, last = max(0, -steps), min(count, count - steps)
    return lax.ppermute(value, "col", [(source, source + steps) for source in range(first, last)])


def steps(matrix):
    place = lax.axis_index("col")
    at_start = place == 0
    at_end = place == lax.axis_size("col") - 1
    ends = jnp.stack([at_start, at_end, lax.axis_index("row_2")]).astype(jnp.int32)
    half, rest = row_halves(*local_gram(ends, matrix))
    top, bottom, right, own_top, own_bottom, own_right, term_0 = rotate(
        True, ends, half, rest, matrix
    )
    from_left = moved(right, 1)
    from_right = moved(bottom, -1)
    own_left = moved(own_right, 1)
    own_from_right = moved(own_bottom, -1)
    pair, cross = local_cross(ends, top, from_left, from_right)
    cross = scattered_sum(cross, ROW)
    cross = gathered(cross, ROW)
    up, inverse = early(ends, own_top, own_left)
    top, bottom, right, terms = rotate(
        False, ends, own_top, own_from_right, up, inverse, cross, pair, term_0
    )
    terms = lax.all_to_all(terms, "col", split_axis=0, concat_axis=0, tiled=True)
    from_left = moved(right, 1)
    from_right = moved(bottom, -1)
    totals = jnp.sum(terms, axis=0)[:STEPS]
    coupling = jnp.sqrt(totals / (1.0 * lax.axis_size("col") * H))
    rotated = placed_blocks(ends, top, from_left, from_right)
    return (rotated, coupling)


def solution(mesh):
    split = Mesh(
        mesh.devices.reshape(8, 2, 2, mesh.shape["col"]), ("row_0", "row_1", "row_2", "col")
    )
    placed = (P(ROW, "col"),)
    return jax.shard_map(steps, mesh=split, in_specs=placed, out_specs=(P(ROW, "col"), P()), check_vma=False)
```

```python
import functools

import jax
import jax.numpy as jnp
from jax import lax
from jax.experimental import pallas as pl
from jax.experimental.pallas import tpu as pltpu
from jax.sharding import Mesh
from jax.sharding import PartitionSpec as P

STEPS = 2
ROW = ("row_0", "row_1", "row_2")
CHIPS = ("row_0", "row_1")
H = 256
TOP = ((0, 0), (0, 1), (1, 1))
CROSS = ((0, 2), (0, 3), (1, 2), (1, 3))
BOTTOM = ((2, 2), (2, 3), (3, 3))
VM = pl.BlockSpec(memory_space=pltpu.VMEM)
SM = pl.BlockSpec(memory_space=pltpu.SMEM)

HI=lax.Precision.HIGHEST
F32=jnp.float32
N=512
T=128
def dot(a,b,ca,cb):
    return lax.dot_general(a,b,(((ca,),(cb,)),((),())),precision=HI,preferred_element_type=F32)
def spread(x): return jnp.broadcast_to(x,(8,T))
def leaves(mats, B=4):
    sub=lax.broadcasted_iota(jnp.int32,(8,T),0); lane=lax.broadcasted_iota(jnp.int32,(8,T),1)
    n=len(mats); G8=T//8
    As=[list(m) for m in mats]
    Is=[[jnp.where(sub+8*q==lane,1.0,0.0).astype(F32) for q in range(G8)] for _ in range(n)]
    for P in range(0,G8,B):
        for p in range(P,P+B):
            r0=8*p
            qs=list(range(p,P+B))
            C=[{q:[spread(A[q][:,r0+k:r0+k+1]) for k in range(8)] for q in qs} for A in As]
            rd=[jnp.ones((8,T),F32) for _ in range(n)]
            for j in range(8):
                for a in range(n):
                    A,I=As[a],Is[a]
                    rinv=1.0/spread(C[a][p][j][j:j+1,:])
                    rd[a]=jnp.where(sub==j,rinv,rd[a])
                    rows=[spread(C[a][p][k][j:j+1,:]) for k in range(j+1,8)]
                    ra=spread(A[p][j:j+1,:]); ri=spread(I[p][j:j+1,:])
                    for q in qs:
                        if q==p:
                            if j==7: continue
                            cm=jnp.where(sub>j,C[a][q][j],0.0)
                            for k in range(j+1,8):
                                C[a][q][k]=C[a][q][k]-(cm*rows[k-j-1])*rinv
                            m=cm*rinv
                        else:
                            m=C[a][q][j]*rinv
                            for k in range(j+1,8):
                                C[a][q][k]=C[a][q][k]-m*rows[k-j-1]
                        A[q]=A[q]-m*ra; I[q]=I[q]-m*ri
            for a in range(n):
                s=jnp.sqrt(rd[a])
                As[a][p]=As[a][p]*s; Is[a][p]=Is[a][p]*s
        if P+B<G8:
            for a in range(n):
                A,I=As[a],Is[a]
                SA=jnp.concatenate(A[P:P+B],axis=0)
                both=jnp.concatenate([SA,jnp.concatenate(I[P:P+B],axis=0)],axis=1)
                upd=dot(SA[:,8*(P+B):],both,0,0)
                for q in range(P+B,G8):
                    o=8*(q-P-B)
                    A[q]=A[q]-upd[o:o+8,:T]; I[q]=I[q]-upd[o:o+8,T:]
    for a in range(n):
        for p in range(G8):
            As[a][p]=jnp.where(lane>=sub+8*p,As[a][p],0.0)
    return As,Is

def tile(ij):
    i,j=ij
    return slice(i*T,(i+1)*T),slice(j*T,(j+1)*T)
def gram_kernel(ends_ref,pair_ref,keep_ref,give_ref,g_ref):
    where={ij:n for n,ij in enumerate(TOP+CROSS+BOTTOM)}
    for i in range(4):
        rows=dot(pair_ref[:,i*T:(i+1)*T],pair_ref[:,i*T:],0,0)
        for j in range(i,4):
            n=where[(i,j)]
            g_ref[n*T:(n+1)*T,:]=rows[:,(j-i)*T:(j-i+1)*T]
    core=ends_ref[2]
    keep_ref[...]=g_ref[pl.ds(pl.multiple_of(core*(5*T),T),5*T),:]
    give_ref[...]=g_ref[pl.ds(pl.multiple_of((1-core)*(5*T),T),5*T),:]
def local_gram(ends,pair):
    half=jax.ShapeDtypeStruct((5*T,T),F32)
    return pl.pallas_call(gram_kernel,out_shape=[half]*2,in_specs=[SM,VM],out_specs=[VM]*2,
        scratch_shapes=[pltpu.VMEM((10*T,T),F32)],compiler_params=pltpu.CompilerParams(vmem_limit_bytes=16 * 2**20),name="gram")(ends,pair)
def cross_kernel(ends_ref,top_ref,from_left_ref,from_right_ref,pair_ref,c_ref):
    own=top_ref[...]
    top=jnp.where(ends_ref[0]==1,own,from_left_ref[...])
    bottom=jnp.where(ends_ref[1]==1,own,from_right_ref[...])
    pair_ref[:,:H]=top
    pair_ref[:,H:]=bottom
    for i in range(2):
        rows=dot(top[:,i*T:(i+1)*T],bottom,0,0)
        c_ref[2*i*T:(2*i+1)*T,:]=rows[:,:T]
        c_ref[(2*i+1)*T:(2*i+2)*T,:]=rows[:,T:]
def local_cross(ends,top,from_left,from_right):
    return pl.pallas_call(cross_kernel,out_shape=[jax.ShapeDtypeStruct((256,512),F32),jax.ShapeDtypeStruct((4*T,T),F32)],
        in_specs=[SM,VM,VM,VM],out_specs=[VM]*2,compiler_params=pltpu.CompilerParams(vmem_limit_bytes=16 * 2**20),name="cross")(ends,top,from_left,from_right)
def spread_leaves(d_ref,u_ref,i_ref,count):
    us,is_=leaves([[d_ref[a,8*q:8*q+8,:] for q in range(T//8)] for a in range(count)])
    for a in range(count):
        for q in range(T//8):
            u_ref[a,8*q:8*q+8,:]=us[a][q]
            i_ref[a,8*q:8*q+8,:]=is_[a][q]
def early_kernel(ends_ref,own_ref,own_left_ref,up_ref,inv_ref,d_ref,u_ref,i_ref):
    g=jnp.where(ends_ref[0]==1,own_ref[...],own_left_ref[...])
    d_ref[0]=g[:T]
    up_ref[T:2*T,:]=g[T:2*T]
    inv_ref[T:2*T,:]=g[2*T:]
    def stage(t,c):
        spread_leaves(d_ref,u_ref,i_ref,1)
        @pl.when(t==0)
        def _():
            up_ref[:T,:]=u_ref[0]
            inv_ref[:T,:]=i_ref[0]
            u01=dot(i_ref[0],up_ref[T:2*T,:],1,0)
            up_ref[T:2*T,:]=u01
            d_ref[0]=inv_ref[T:2*T,:]-dot(u01,u01,0,0)
        @pl.when(t==1)
        def _():
            up_ref[2*T:,:]=u_ref[0]
            inv_ref[2*T:,:]=i_ref[0]
            inv_ref[T:2*T,:]=-dot(i_ref[0],dot(up_ref[T:2*T,:],inv_ref[:T,:],0,0),1,0)
        return c
    lax.fori_loop(0,2,stage,0)
def early(*operands):
    own=jax.ShapeDtypeStruct((3*T,T),F32)
    return pl.pallas_call(early_kernel,out_shape=[own]*2,in_specs=[SM,VM,VM],out_specs=[VM]*2,
        scratch_shapes=[pltpu.VMEM((1,T,T),F32)]*3,
        cost_estimate=pl.CostEstimate(flops=500_000_000,bytes_accessed=1_000_000,transcendentals=0),
        compiler_params=pltpu.CompilerParams(vmem_limit_bytes=16 * 2**20),name="early")(*operands)
def coupling_sum(A,down,along):
    cpl=jnp.zeros((1,T),F32)
    for i in (0,1):
        for j in (2,3):
            c=A[tile((i,j))]
            cpl=cpl+jnp.sum(c*c/(down[i]*along[j-2]),axis=0,keepdims=True)
    return jnp.broadcast_to(jnp.sum(cpl,axis=1,keepdims=True),(8,T))
def rotate_kernel(first,*refs):
    if first:
        ends_ref,half_ref,rest_ref,pair_ref,top_ref,bottom_ref,right_ref,own_top_ref,own_bottom_ref,own_right_ref,cpl_ref=refs[:11]
        refs=refs[11:]
    else:
        ends_ref,own_ref,own_from_right_ref,up_ref,inv_ref,g_ref,pair_ref,term_ref,top_ref,bottom_ref,right_ref,cpl_ref=refs[:12]
        refs=refs[12:]
    A,U,V,W,RT,d_ref,u_ref,i_ref=refs
    sub=lax.broadcasted_iota(jnp.int32,(T,T),0); lane=lax.broadcasted_iota(jnp.int32,(T,T),1)
    eye=sub==lane
    U[...]=jnp.zeros_like(U); V[...]=jnp.zeros_like(V)
    def along_of(n):
        return jnp.sum(jnp.where(eye,A[tile((n,n))],0.0),axis=0,keepdims=True)
    def down_of(row):
        return jnp.sum(jnp.where(eye,row,0.0),axis=1,keepdims=True)
    def next_d2(t):
        lo,hi=t*T,(t+1)*T
        bcol=dot(U[:hi,lo:],U[lo:hi,lo:],1,1)
        if t:
            vcol=dot(W[:lo,:lo],bcol[:lo],1,0)
            V[:lo,lo:hi]=vcol
            d_ref[1]=bcol[lo:]-dot(vcol,vcol,0,0)
        else:
            d_ref[1]=bcol
    def inner_part(s):
        sl,sh=s*T,(s+1)*T
        V[sl:sh,sl:sh]=u_ref[1]
        sinv=i_ref[1]
        W[sl:sh,sl:sh]=sinv
        if s:
            t1=dot(V[:sl,sl:sh],W[:sl,:sl],0,0)
            W[sl:sh,:sl]=-dot(sinv,t1,1,0)
            W[:sl,sl:sh]=jnp.zeros((sl,T),F32)
    def outer_part(t):
        lo,hi=t*T,(t+1)*T
        U[lo:hi,lo:hi]=u_ref[0]
        if t<3:
            U[lo:hi,hi:]=dot(i_ref[0],A[lo:hi,hi:],1,0)
            d_ref[0]=A[hi:hi+T,hi:hi+T]-dot(U[lo:hi,hi:hi+T],U[lo:hi,hi:hi+T],0,0)
    def trailing(t):
        lo,hi=t*T,(t+1)*T
        for i in range(t+1,4):
            a,b=i*T,(i+1)*T
            A[a:b,a:]=A[a:b,a:]-dot(U[lo:hi,a:b],U[lo:hi,a:],0,0)
    def turn_row(s):
        sl,sh=s*T,(s+1)*T
        RT[sl:sh,:]=dot(W[sl:sh,:sh],U[:sh,:],1,0)
    if first:
        for n,ij in enumerate(TOP+CROSS+BOTTOM):
            m=(n%5)*T
            A[tile(ij)]=jnp.where(ends_ref[2]==n//5,half_ref[m:m+T,:],rest_ref[m:m+T,:])
        d_ref[0]=A[:T,:T]
        d_ref[1]=jnp.where(eye,1.0,0.0).astype(F32)
        down=[down_of(A[tile((n,n))]) for n in (0,1)]
        skip=0
    else:
        own_bottom=jnp.where(ends_ref[1]==1,own_ref[...],own_from_right_ref[...])
        for n in range(3):
            A[tile(BOTTOM[n])]=own_bottom[n*T:(n+1)*T]
            U[tile(TOP[n])]=up_ref[n*T:(n+1)*T,:]
        for n,ij in enumerate(CROSS):
            A[tile(ij)]=g_ref[n*T:(n+1)*T,:]
        sq=[jnp.sum(up_ref[n*T:(n+1)*T,:]*up_ref[n*T:(n+1)*T,:],axis=0,keepdims=True) for n in range(3)]
        down=[down_of(sq[0]),down_of(sq[1]+sq[2])]
        skip=2
    term=coupling_sum(A,down,[along_of(2),along_of(3)])
    if first:
        cpl_ref[...]=term
    else:
        cpl_ref[...]=jnp.where(lane[:8]==0,term_ref[...],term)
    if not first:
        U[:T,H:]=dot(inv_ref[:T,:],A[:T,H:],1,0)
        U[T:H,H:]=dot(inv_ref[T:2*T,:],A[:T,H:],1,0)+dot(inv_ref[2*T:,:],A[T:H,H:],1,0)
        for a in (H,H+T):
            A[a:a+T,a:]=A[a:a+T,a:]-dot(U[:H,a:a+T],U[:H,a:],0,0)
        d_ref[0]=A[H:H+T,H:H+T]
        next_d2(0)
    def branch(k):
        s=k-1 if first else k
        t=k+skip
        if s>=0:
            inner_part(s)
        if t<4:
            outer_part(t)
        if s+1<4:
            next_d2(s+1)
        if t<4:
            trailing(t)
        if s>=0:
            turn_row(s)
    stages=5 if first else 4
    def stage(t,c):
        spread_leaves(d_ref,u_ref,i_ref,2)
        for k in range(stages):
            pl.when(t==k)(functools.partial(branch,k))
        return c
    lax.fori_loop(0,stages,stage,0)
    turned=dot(pair_ref[...],RT[...],1,1)
    top,bottom=turned[:,:H],turned[:,H:]
    top_ref[...]=top
    bottom_ref[...]=bottom
    at_start=ends_ref[0]==1
    right_ref[...]=jnp.where(at_start,bottom,top)
    if first:
        def packed(ref,lo):
            a=dot(V[lo:lo+T,lo:],V[lo:lo+H,lo:],1,1)
            b=dot(V[lo+T:lo+H,lo:],V[lo+T:lo+H,lo:],1,1)
            ref[:T,:]=a[:,:T]
            ref[T:2*T,:]=a[:,T:]
            ref[2*T:,:]=b
        packed(own_top_ref,0)
        packed(own_bottom_ref,H)
        own_right_ref[...]=jnp.where(at_start,own_bottom_ref[...],own_top_ref[...])
def rotate(first,*operands):
    block=jax.ShapeDtypeStruct((256,H),F32)
    own=jax.ShapeDtypeStruct((3*T,T),F32)
    outs=[block]*3+([own]*3 if first else [])+[jax.ShapeDtypeStruct((8,T),F32)]
    return pl.pallas_call(functools.partial(rotate_kernel,first),out_shape=outs,
        in_specs=[SM]+[VM]*(len(operands)-1),out_specs=[VM]*len(outs),
        scratch_shapes=[pltpu.VMEM((N,N),F32)]*5+[pltpu.VMEM((2,T,T),F32)]*3,
        cost_estimate=pl.CostEstimate(flops=4_000_000_000,bytes_accessed=2_000_000,transcendentals=0),
        compiler_params=pltpu.CompilerParams(vmem_limit_bytes=32 * 2**20),name="rotate")(*operands)


def scattered_sum(value, axis):
    count = lax.axis_size(axis)
    parts = lax.all_to_all(value.reshape(count, -1, T), axis, 0, 0, tiled=True)
    return jnp.sum(parts, axis=0)


def gathered(value, axis):
    copies = jnp.broadcast_to(value, (lax.axis_size(axis), *value.shape))
    return lax.all_to_all(copies, axis, split_axis=0, concat_axis=0, tiled=True).reshape(-1, T)


def swapped(value):
    return lax.ppermute(value, "row_2", [(0, 1), (1, 0)])


def row_halves(keep, give):
    half = gathered(scattered_sum(keep + swapped(give), CHIPS), CHIPS)
    return half, swapped(half)


def moved(value, steps):
    count = lax.axis_size("col")
    first, last = max(0, -steps), min(count, count - steps)
    return lax.ppermute(value, "col", [(source, source + steps) for source in range(first, last)])


def steps(matrix):
    place = lax.axis_index("col")
    at_start = place == 0
    at_end = place == lax.axis_size("col") - 1
    ends = jnp.stack([at_start, at_end, lax.axis_index("row_2")]).astype(jnp.int32)
    half, rest = row_halves(*local_gram(ends, matrix))
    top, bottom, right, own_top, own_bottom, own_right, term_0 = rotate(
        True, ends, half, rest, matrix
    )
    from_left = moved(right, 1)
    from_right = moved(bottom, -1)
    own_left = moved(own_right, 1)
    own_from_right = moved(own_bottom, -1)
    pair, cross = local_cross(ends, top, from_left, from_right)
    cross = scattered_sum(cross, ROW)
    cross = gathered(cross, ROW)
    up, inverse = early(ends, own_top, own_left)
    top, bottom, right, terms = rotate(
        False, ends, own_top, own_from_right, up, inverse, cross, pair, term_0
    )
    terms = lax.all_to_all(terms, "col", split_axis=0, concat_axis=0, tiled=True)
    from_left = moved(right, 1)
    from_right = moved(bottom, -1)
    totals = jnp.sum(terms, axis=0)[:STEPS]
    coupling = jnp.sqrt(totals / (1.0 * lax.axis_size("col") * H))
    rotated = jnp.concatenate(
        [jnp.where(at_start, top, from_left), jnp.where(at_end, top, from_right)], axis=1
    )
    return (rotated, coupling)


def solution(mesh):
    split = Mesh(
        mesh.devices.reshape(8, 2, 2, mesh.shape["col"]), ("row_0", "row_1", "row_2", "col")
    )
    placed = (P(ROW, "col"),)
    return jax.shard_map(steps, mesh=split, in_specs=placed, out_specs=(P(ROW, "col"), P()), check_vma=False)
```

```python
import functools

import jax
import jax.numpy as jnp
from jax import lax
from jax.experimental import pallas as pl
from jax.experimental.pallas import tpu as pltpu
from jax.sharding import Mesh
from jax.sharding import PartitionSpec as P

STEPS = 2
ROW = ("row_0", "row_1", "row_2")
CHIPS = ("row_0", "row_1")
H = 256
TOP = ((0, 0), (0, 1), (1, 1))
CROSS = ((0, 2), (0, 3), (1, 2), (1, 3))
BOTTOM = ((2, 2), (2, 3), (3, 3))
VM = pl.BlockSpec(memory_space=pltpu.VMEM)
SM = pl.BlockSpec(memory_space=pltpu.SMEM)

HI=lax.Precision.HIGHEST
F32=jnp.float32
N=512
T=128
def dot(a,b,ca,cb):
    return lax.dot_general(a,b,(((ca,),(cb,)),((),())),precision=HI,preferred_element_type=F32)
def spread(x): return jnp.broadcast_to(x,(8,T))
def leaves(mats, B=4):
    sub=lax.broadcasted_iota(jnp.int32,(8,T),0); lane=lax.broadcasted_iota(jnp.int32,(8,T),1)
    n=len(mats); G8=T//8
    As=[list(m) for m in mats]
    Is=[[jnp.where(sub+8*q==lane,1.0,0.0).astype(F32) for q in range(G8)] for _ in range(n)]
    for P in range(0,G8,B):
        for p in range(P,P+B):
            r0=8*p
            qs=list(range(p,P+B))
            C=[{q:[spread(A[q][:,r0+k:r0+k+1]) for k in range(8)] for q in qs} for A in As]
            rd=[jnp.ones((8,T),F32) for _ in range(n)]
            for j in range(8):
                for a in range(n):
                    A,I=As[a],Is[a]
                    rinv=1.0/spread(C[a][p][j][j:j+1,:])
                    rd[a]=jnp.where(sub==j,rinv,rd[a])
                    rows=[spread(C[a][p][k][j:j+1,:]) for k in range(j+1,8)]
                    ra=spread(A[p][j:j+1,:]); ri=spread(I[p][j:j+1,:])
                    for q in qs:
                        if q==p:
                            if j==7: continue
                            cm=jnp.where(sub>j,C[a][q][j],0.0)
                            for k in range(j+1,8):
                                C[a][q][k]=C[a][q][k]-(cm*rows[k-j-1])*rinv
                            m=cm*rinv
                        else:
                            m=C[a][q][j]*rinv
                            for k in range(j+1,8):
                                C[a][q][k]=C[a][q][k]-m*rows[k-j-1]
                        A[q]=A[q]-m*ra; I[q]=I[q]-m*ri
            for a in range(n):
                s=jnp.sqrt(rd[a])
                As[a][p]=As[a][p]*s; Is[a][p]=Is[a][p]*s
        if P+B<G8:
            for a in range(n):
                A,I=As[a],Is[a]
                SA=jnp.concatenate(A[P:P+B],axis=0)
                both=jnp.concatenate([SA,jnp.concatenate(I[P:P+B],axis=0)],axis=1)
                upd=dot(SA[:,8*(P+B):],both,0,0)
                for q in range(P+B,G8):
                    o=8*(q-P-B)
                    A[q]=A[q]-upd[o:o+8,:T]; I[q]=I[q]-upd[o:o+8,T:]
    for a in range(n):
        for p in range(G8):
            As[a][p]=jnp.where(lane>=sub+8*p,As[a][p],0.0)
    return As,Is

def tile(ij):
    i,j=ij
    return slice(i*T,(i+1)*T),slice(j*T,(j+1)*T)
def gram_kernel(ends_ref,pair_ref,keep_ref,give_ref,g_ref):
    where={ij:n for n,ij in enumerate(TOP+CROSS+BOTTOM)}
    for i in range(4):
        rows=dot(pair_ref[:,i*T:(i+1)*T],pair_ref[:,i*T:],0,0)
        for j in range(i,4):
            n=where[(i,j)]
            g_ref[n*T:(n+1)*T,:]=rows[:,(j-i)*T:(j-i+1)*T]
    core=ends_ref[2]
    keep_ref[...]=g_ref[pl.ds(pl.multiple_of(core*(5*T),T),5*T),:]
    give_ref[...]=g_ref[pl.ds(pl.multiple_of((1-core)*(5*T),T),5*T),:]
def local_gram(ends,pair):
    half=jax.ShapeDtypeStruct((5*T,T),F32)
    return pl.pallas_call(gram_kernel,out_shape=[half]*2,in_specs=[SM,VM],out_specs=[VM]*2,
        scratch_shapes=[pltpu.VMEM((10*T,T),F32)],compiler_params=pltpu.CompilerParams(vmem_limit_bytes=16 * 2**20),name="gram")(ends,pair)
def cross_kernel(ends_ref,keep_ref,far_ref,edge_ref,pair_ref,hold_ref,give_ref):
    edge=edge_ref[...]
    top=jnp.where(ends_ref[1]==1,edge,keep_ref[...])
    bottom=jnp.where(ends_ref[3]==1,edge,far_ref[...])
    pair_ref[:,:H]=top
    pair_ref[:,H:]=bottom
    low=ends_ref[2]==0
    upper=dot(top[:,:T],bottom,0,0)
    lower=dot(top[:,T:],bottom,0,0)
    hold=jnp.where(low,upper,lower)
    give=jnp.where(low,lower,upper)
    for j in range(2):
        hold_ref[j*T:(j+1)*T,:]=hold[:,j*T:(j+1)*T]
        give_ref[j*T:(j+1)*T,:]=give[:,j*T:(j+1)*T]
def local_cross(*operands):
    half=jax.ShapeDtypeStruct((2*T,T),F32)
    return pl.pallas_call(cross_kernel,out_shape=[jax.ShapeDtypeStruct((256,512),F32),half,half],
        in_specs=[SM,VM,VM,VM],out_specs=[VM]*3,compiler_params=pltpu.CompilerParams(vmem_limit_bytes=16 * 2**20),name="cross")(*operands)
def spread_leaves(d_ref,u_ref,i_ref,count):
    us,is_=leaves([[d_ref[a,8*q:8*q+8,:] for q in range(T//8)] for a in range(count)])
    for a in range(count):
        for q in range(T//8):
            u_ref[a,8*q:8*q+8,:]=us[a][q]
            i_ref[a,8*q:8*q+8,:]=is_[a][q]
def early_kernel(ends_ref,own_keep_ref,own_edge_ref,up_ref,inv_ref,d_ref,u_ref,i_ref):
    g=jnp.where(ends_ref[1]==1,own_edge_ref[...],own_keep_ref[...])
    d_ref[0]=g[:T]
    up_ref[T:2*T,:]=g[T:2*T]
    inv_ref[T:2*T,:]=g[2*T:]
    def stage(t,c):
        spread_leaves(d_ref,u_ref,i_ref,1)
        @pl.when(t==0)
        def _():
            up_ref[:T,:]=u_ref[0]
            inv_ref[:T,:]=i_ref[0]
            u01=dot(i_ref[0],up_ref[T:2*T,:],1,0)
            up_ref[T:2*T,:]=u01
            d_ref[0]=inv_ref[T:2*T,:]-dot(u01,u01,0,0)
        @pl.when(t==1)
        def _():
            up_ref[2*T:,:]=u_ref[0]
            inv_ref[2*T:,:]=i_ref[0]
            inv_ref[T:2*T,:]=-dot(i_ref[0],dot(up_ref[T:2*T,:],inv_ref[:T,:],0,0),1,0)
        return c
    lax.fori_loop(0,2,stage,0)
def early(*operands):
    own=jax.ShapeDtypeStruct((3*T,T),F32)
    return pl.pallas_call(early_kernel,out_shape=[own]*2,in_specs=[SM,VM,VM],out_specs=[VM]*2,
        scratch_shapes=[pltpu.VMEM((1,T,T),F32)]*3,
        cost_estimate=pl.CostEstimate(flops=500_000_000,bytes_accessed=1_000_000,transcendentals=0),
        compiler_params=pltpu.CompilerParams(vmem_limit_bytes=16 * 2**20),name="early")(*operands)
def coupling_sum(A,down,along):
    cpl=jnp.zeros((1,T),F32)
    for i in (0,1):
        for j in (2,3):
            c=A[tile((i,j))]
            cpl=cpl+jnp.sum(c*c/(down[i]*along[j-2]),axis=0,keepdims=True)
    return jnp.broadcast_to(jnp.sum(cpl,axis=1,keepdims=True),(8,T))
def rotate_kernel(first,*refs):
    if first:
        ends_ref,half_ref,rest_ref,pair_ref,top_ref,bottom_ref,pick_ref,own_top_ref,own_bottom_ref,own_pick_ref,cpl_ref=refs[:11]
        refs=refs[11:]
    else:
        ends_ref,own_edge_ref,own_far_ref,up_ref,inv_ref,half_ref,rest_ref,pair_ref,term_ref,top_ref,bottom_ref,pick_ref,cpl_ref=refs[:13]
        refs=refs[13:]
    A,U,V,W,RT,d_ref,u_ref,i_ref=refs
    sub=lax.broadcasted_iota(jnp.int32,(T,T),0); lane=lax.broadcasted_iota(jnp.int32,(T,T),1)
    eye=sub==lane
    U[...]=jnp.zeros_like(U); V[...]=jnp.zeros_like(V)
    def along_of(n):
        return jnp.sum(jnp.where(eye,A[tile((n,n))],0.0),axis=0,keepdims=True)
    def down_of(row):
        return jnp.sum(jnp.where(eye,row,0.0),axis=1,keepdims=True)
    def next_d2(t):
        lo,hi=t*T,(t+1)*T
        bcol=dot(U[:hi,lo:],U[lo:hi,lo:],1,1)
        if t:
            vcol=dot(W[:lo,:lo],bcol[:lo],1,0)
            V[:lo,lo:hi]=vcol
            d_ref[1]=bcol[lo:]-dot(vcol,vcol,0,0)
        else:
            d_ref[1]=bcol
    def inner_part(s):
        sl,sh=s*T,(s+1)*T
        V[sl:sh,sl:sh]=u_ref[1]
        sinv=i_ref[1]
        W[sl:sh,sl:sh]=sinv
        if s:
            t1=dot(V[:sl,sl:sh],W[:sl,:sl],0,0)
            W[sl:sh,:sl]=-dot(sinv,t1,1,0)
            W[:sl,sl:sh]=jnp.zeros((sl,T),F32)
    def outer_part(t):
        lo,hi=t*T,(t+1)*T
        U[lo:hi,lo:hi]=u_ref[0]
        if t<3:
            U[lo:hi,hi:]=dot(i_ref[0],A[lo:hi,hi:],1,0)
            d_ref[0]=A[hi:hi+T,hi:hi+T]-dot(U[lo:hi,hi:hi+T],U[lo:hi,hi:hi+T],0,0)
    def trailing(t):
        lo,hi=t*T,(t+1)*T
        for i in range(t+1,4):
            a,b=i*T,(i+1)*T
            A[a:b,a:]=A[a:b,a:]-dot(U[lo:hi,a:b],U[lo:hi,a:],0,0)
    def turn_row(s):
        sl,sh=s*T,(s+1)*T
        RT[sl:sh,:]=dot(W[sl:sh,:sh],U[:sh,:],1,0)
    if first:
        for n,ij in enumerate(TOP+CROSS+BOTTOM):
            m=(n%5)*T
            A[tile(ij)]=jnp.where(ends_ref[2]==n//5,half_ref[m:m+T,:],rest_ref[m:m+T,:])
        d_ref[0]=A[:T,:T]
        d_ref[1]=jnp.where(eye,1.0,0.0).astype(F32)
        down=[down_of(A[tile((n,n))]) for n in (0,1)]
        skip=0
    else:
        own_bottom=jnp.where(ends_ref[3]==1,own_edge_ref[...],own_far_ref[...])
        for n in range(3):
            A[tile(BOTTOM[n])]=own_bottom[n*T:(n+1)*T]
            U[tile(TOP[n])]=up_ref[n*T:(n+1)*T,:]
        for n,ij in enumerate(CROSS):
            m=(n%2)*T
            A[tile(ij)]=jnp.where(ends_ref[2]==n//2,half_ref[m:m+T,:],rest_ref[m:m+T,:])
        sq=[jnp.sum(up_ref[n*T:(n+1)*T,:]*up_ref[n*T:(n+1)*T,:],axis=0,keepdims=True) for n in range(3)]
        down=[down_of(sq[0]),down_of(sq[1]+sq[2])]
        skip=2
    term=coupling_sum(A,down,[along_of(2),along_of(3)])
    if first:
        cpl_ref[...]=term
    else:
        cpl_ref[...]=jnp.where(lane[:8]==0,term_ref[...],term)
    if not first:
        U[:T,H:]=dot(inv_ref[:T,:],A[:T,H:],1,0)
        U[T:H,H:]=dot(inv_ref[T:2*T,:],A[:T,H:],1,0)+dot(inv_ref[2*T:,:],A[T:H,H:],1,0)
        for a in (H,H+T):
            A[a:a+T,a:]=A[a:a+T,a:]-dot(U[:H,a:a+T],U[:H,a:],0,0)
        d_ref[0]=A[H:H+T,H:H+T]
        next_d2(0)
    def branch(k):
        s=k-1 if first else k
        t=k+skip
        if s>=0:
            inner_part(s)
        if t<4:
            outer_part(t)
        if s+1<4:
            next_d2(s+1)
        if t<4:
            trailing(t)
        if s>=0:
            turn_row(s)
    stages=5 if first else 4
    def stage(t,c):
        spread_leaves(d_ref,u_ref,i_ref,2)
        for k in range(stages):
            pl.when(t==k)(functools.partial(branch,k))
        return c
    lax.fori_loop(0,stages,stage,0)
    turned=dot(pair_ref[...],RT[...],1,1)
    top,bottom=turned[:,:H],turned[:,H:]
    top_ref[...]=top
    bottom_ref[...]=bottom
    swap=ends_ref[0 if first else 1]==1
    pick_ref[...]=jnp.where(swap,bottom,top)
    if first:
        def packed(ref,lo):
            a=dot(V[lo:lo+T,lo:],V[lo:lo+H,lo:],1,1)
            b=dot(V[lo+T:lo+H,lo:],V[lo+T:lo+H,lo:],1,1)
            ref[:T,:]=a[:,:T]
            ref[T:2*T,:]=a[:,T:]
            ref[2*T:,:]=b
        packed(own_top_ref,0)
        packed(own_bottom_ref,H)
        own_pick_ref[...]=jnp.where(swap,own_bottom_ref[...],own_top_ref[...])
def rotate(first,*operands):
    block=jax.ShapeDtypeStruct((256,H),F32)
    own=jax.ShapeDtypeStruct((3*T,T),F32)
    outs=[block]*3+([own]*3 if first else [])+[jax.ShapeDtypeStruct((8,T),F32)]
    return pl.pallas_call(functools.partial(rotate_kernel,first),out_shape=outs,
        in_specs=[SM]+[VM]*(len(operands)-1),out_specs=[VM]*len(outs),
        scratch_shapes=[pltpu.VMEM((N,N),F32)]*5+[pltpu.VMEM((2,T,T),F32)]*3,
        cost_estimate=pl.CostEstimate(flops=4_000_000_000,bytes_accessed=2_000_000,transcendentals=0),
        compiler_params=pltpu.CompilerParams(vmem_limit_bytes=32 * 2**20),name="rotate")(*operands)


def scattered_sum(value, axis):
    count = lax.axis_size(axis)
    parts = lax.all_to_all(value.reshape(count, -1, T), axis, 0, 0, tiled=True)
    return jnp.sum(parts, axis=0)


def gathered(value, axis):
    copies = jnp.broadcast_to(value, (lax.axis_size(axis), *value.shape))
    return lax.all_to_all(copies, axis, split_axis=0, concat_axis=0, tiled=True).reshape(-1, T)


def swapped(value):
    return lax.ppermute(value, "row_2", [(0, 1), (1, 0)])


def row_halves(keep, give):
    half = gathered(scattered_sum(keep + swapped(give), CHIPS), CHIPS)
    return half, swapped(half)


def moved(value, steps, sources):
    count = lax.axis_size("col")
    return lax.ppermute(value, "col", [(i % count, (i + steps) % count) for i in sources])


def carried(value, links):
    return lax.ppermute(value, "col", links)


def steps(matrix):
    place = lax.axis_index("col")
    count = lax.axis_size("col")
    last = count - 1
    ends = jnp.stack(
        [place == 0, place == last, lax.axis_index("row_2"), place == last - 1]
    ).astype(jnp.int32)
    half, rest = row_halves(*local_gram(ends, matrix))
    top, bottom, keep, own_top, own_bottom, own_keep, term_0 = rotate(
        True, ends, half, rest, matrix
    )
    edges = [(last, last - 1), (0, last)]
    far = moved(bottom, -2, range(1, count))
    edge = carried(top, edges)
    own_far = moved(own_bottom, -2, range(1, count))
    own_edge = carried(own_top, edges)
    pair, hold, give = local_cross(ends, keep, far, edge)
    cross = scattered_sum(hold + swapped(give), CHIPS)
    cross = gathered(cross, CHIPS)
    cross_rest = swapped(cross)
    up, inverse = early(ends, own_keep, own_edge)
    top, bottom, pick, terms = rotate(
        False, ends, own_edge, own_far, up, inverse, cross, cross_rest, pair, term_0
    )
    far = moved(pick, 2, [*range(last - 1), last])
    edge = carried(top, [(last - 1, last), (last, 0)])
    terms = lax.all_to_all(terms, "col", split_axis=0, concat_axis=0, tiled=True)
    totals = jnp.sum(terms, axis=0)[:STEPS]
    coupling = jnp.sqrt(totals / (1.0 * count * H))
    rotated = jnp.concatenate(
        [jnp.where(place == 0, edge, far), jnp.where(place == last, edge, bottom)], axis=1
    )
    return (rotated, coupling)


def solution(mesh):
    split = Mesh(
        mesh.devices.reshape(8, 2, 2, mesh.shape["col"]), ("row_0", "row_1", "row_2", "col")
    )
    placed = (P(ROW, "col"),)
    return jax.shard_map(
        steps, mesh=split, in_specs=placed, out_specs=(P(ROW, "col"), P()), check_vma=False
    )
```
